256 devices in a mesh: grp: 8 (over y, x_lo), brick: 32 (over z, x_hi, core).
Axes of the slice: x: 4 (x_hi: 2, x_lo: 2; x = x_hi * 2 + x_lo), y: 4, z: 8, core: 2. Of those that a mesh axis runs over, the one named last changes fastest.
Arguments:
- coeffs: bfloat16 [8, 16384, 1024], P(None, 'brick'), may hold values from -6 to 6
- tensor: bfloat16 [32, 1024, 1024], P('grp', 'brick'), may hold values from -0.005859375 to 0.005859375
- pairs: int32 [2, 2], replicated, may hold values from 0 to 7
- lateral: int32 [16384], P('brick'), may hold values from 0 to 511
- thermal: float32 [8], replicated, may hold values from 0.5 to 1
Outputs:
- updated: float32 [32, 8, 16384], P(None, None, 'brick')
The draws below stay inside these ranges and needn't reach their ends.
Inputs may be any that keep to these rules, and one draw needn't show every extreme that they name: `pairs`: row p names the species that receives the collision term and the species it collides with. A cell's lateral partner, as an index within the same block of 512 cells.
All inputs are finite; a program needn't handle non-finite values.
Results may differ from the reference program's by a relative error of at most 0.0003.
Values may be sent and summed in bfloat16 or wider, within the bound.
No kernel may reach another device: no remote copies, remote signals or barrier semaphores. Data moves between devices by JAX's collectives and lax.ppermute only.
A program may use at most 128 MiB of HBM per device.

```python
import math
import jax
import jax.numpy as jnp
from jax import lax

M = 1024
MODES = 32
SPECIES = 8
PAIRS = 2
PLANE = 128
C_DEV = 512
CELLS = 16384


def set_ends(result, stream_key, least, high):
    dims = result.shape
    spot = [jax.random.randint(jax.random.fold_in(stream_key, axis), (), 0, dims[axis]) for axis in range(len(dims))]
    result = result.at[tuple(spot)].set(least)
    longest = dims.index(max(dims))
    spot[longest] = (spot[longest] + 1) % dims[longest]
    return result.at[tuple(spot)].set(high)


def block_levels(rng, shape, shards, least, largest):
    def one(position, blocks):
        draws = jax.random.uniform(jax.random.fold_in(jax.random.fold_in(rng, 6), position), (blocks,), jnp.float32, least / len(shards), largest / len(shards))
        return jnp.repeat(jnp.exp(draws), shape[position] // blocks).reshape((-1,) + (1,) * (len(shape) - position - 1))

    level = one(*shards[0])
    for cut in shards[1:]:
        level = level * one(*cut)
    return level


def bell_draw(own_key, dims, scale, reach, pieces=(), kind=jnp.bfloat16):
    entries = scale * jax.random.normal(own_key, dims, jnp.float32)
    if pieces:
        entries = entries * block_levels(own_key, dims, pieces, -0.22, 0.18)
    return jnp.clip(entries, -reach, reach).astype(kind)


def setup_inputs(seed: int = 0) -> dict:
    arg_keys = jax.random.split(jax.random.key(seed), 6)
    coeffs = bell_draw(arg_keys[0], (SPECIES, CELLS, M), 1.0, 6.0, ((1, 32),))
    tensor = bell_draw(arg_keys[1], (MODES, M, M), (M * M) ** -0.5, 0.005859375, ((0, 8), (1, 32)))
    pairs = set_ends(jax.random.randint(arg_keys[2], (PAIRS, 2), 0, SPECIES), jax.random.fold_in(arg_keys[2], 1), 0, SPECIES - 1).astype(jnp.int32)
    lateral = set_ends(jax.random.randint(arg_keys[3], (CELLS,), 0, C_DEV), jax.random.fold_in(arg_keys[3], 1), 0, C_DEV - 1).astype(jnp.int32)
    thermal = jnp.clip(jnp.exp(jax.random.uniform(arg_keys[4], (SPECIES,), jnp.float32, math.log(0.5), math.log(1.0))), 0.5, 1.0)
    return {"coeffs": coeffs, "tensor": tensor, "pairs": pairs, "lateral": lateral, "thermal": thermal}


collision_update = 0.5
courant = 0.08
max_speed = 11.0
mixing = 0.2

def advance(extended, first_mode, thermal, partner):
    mode_count = extended.shape[0] - 2
    thermo = thermal[None, :, None, None]
    orders = (first_mode + jnp.arange(mode_count, dtype=jnp.int32)).astype(jnp.float32)[:, None, None, None]
    speed = thermo * (jnp.sqrt(orders) * extended[:mode_count] + jnp.sqrt(orders + 1.0) * extended[2:])
    middle = extended[1:mode_count + 1]
    face = 0.5 * (speed[:, :, :-1] + speed[:, :, 1:]) - 0.5 * max_speed * thermo * (middle[:, :, 1:] - middle[:, :, :-1])
    center = middle[:, :, 1:-1]
    shape_flat = (mode_count, center.shape[1], center.shape[2] * center.shape[3])
    center = center.reshape(shape_flat)
    divergence = (face[:, :, 1:] - face[:, :, :-1]).reshape(shape_flat)
    beside = jnp.take(center, partner, axis=2)
    return center - courant * divergence + mixing * (beside - center)

def reference(coeffs, tensor, pairs, lateral, thermal):
    species, cells, width = coeffs.shape
    modes = tensor.shape[0]
    pair_count = pairs.shape[0]
    left_side = coeffs[pairs[:, 0]].astype(jnp.float32).reshape(pair_count * cells, width)
    right_side = coeffs[pairs[:, 1]].astype(jnp.float32).reshape(pair_count * cells, width)

    def one_mode(slab):
        inner = jnp.dot(right_side, slab.astype(jnp.float32).T, precision=lax.Precision.HIGHEST)
        return lax.optimization_barrier(jnp.sum(left_side * inner, axis=1))
    collide = lax.map(one_mode, tensor).reshape(modes, pair_count, cells)
    indicator_matrix = (pairs[:, 0][:, None] == jnp.arange(species, dtype=jnp.int32)[None, :]).astype(jnp.float32)
    collision_operator = jnp.einsum('quw,ut->qtw', collide, indicator_matrix, precision=lax.Precision.HIGHEST)
    brick_window = jnp.transpose(coeffs[:, :, :modes], (2, 0, 1))
    species_state = brick_window.astype(jnp.float32) + collision_update * collision_operator
    species_state = jnp.pad(species_state, ((1, 1), (0, 0), (0, 0)))
    layers = cells // PLANE
    species_state = species_state.reshape(modes + 2, species, layers, PLANE)
    extended = jnp.concatenate([species_state[:, :, -1:], species_state, species_state[:, :, :1]], axis=2)
    cell_index = jnp.arange(cells, dtype=jnp.int32)
    partner = (cell_index // C_DEV * C_DEV + lateral).astype(jnp.int32)
    return advance(extended, jnp.int32(0), thermal, partner)
```

```python
import functools

import jax
import jax.numpy as jnp
from jax import lax
from jax.experimental import pallas as pl
from jax.experimental.pallas import tpu as pltpu
from jax.sharding import Mesh, PartitionSpec as P

PLANE = 128
Y, XL, Z, XH, CORE = 4, 2, 8, 2, 2
FINE = ("y", "xl", "z", "xh", "core")
BRICK = ("z", "xh", "core")
MODES_HERE = 4
ROWS = 32

collision_update = 0.5
courant = 0.08
max_speed = 11.0
mixing = 0.2

UP = [(i, (i + 1) % Z) for i in range(Z)]
DOWN = [((i + 1) % Z, i) for i in range(Z)]
SWAP = [(0, 1), (1, 0)]


def prepare_kernel(place, pairs, left, right, right_out, keep, send):
    core = place[2]
    right_out[...] = right[...]
    turned = jnp.transpose(left[0]).reshape(Z * XH, CORE, ROWS, left.shape[1])

    @pl.when(core == 0)
    def _():
        keep[0] = turned[:, 0]
        send[0] = turned[:, 1]

    @pl.when(core == 1)
    def _():
        keep[0] = turned[:, 1]
        send[0] = turned[:, 0]


def prepare(place, pairs, coeffs):
    _, cells, width = coeffs.shape
    halves = jax.ShapeDtypeStruct((2, Z * XH, ROWS, cells), coeffs.dtype)
    half_spec = pl.BlockSpec((1, Z * XH, ROWS, cells), lambda p, place, pairs: (p, 0, 0, 0))
    return pl.pallas_call(
        prepare_kernel,
        grid_spec=pltpu.PrefetchScalarGridSpec(
            num_scalar_prefetch=2,
            grid=(2,),
            in_specs=[
                pl.BlockSpec((1, cells, width), lambda p, place, pairs: (pairs[p, 0], 0, 0)),
                pl.BlockSpec((1, cells, width), lambda p, place, pairs: (pairs[p, 1], 0, 0)),
            ],
            out_specs=[
                pl.BlockSpec((1, cells, width), lambda p, place, pairs: (p, 0, 0)),
                half_spec,
                half_spec,
            ],
        ),
        out_shape=[jax.ShapeDtypeStruct((2, cells, width), coeffs.dtype), halves, halves],
        compiler_params=pltpu.CompilerParams(vmem_limit_bytes=40 * 2**20),
        name="prepare",
    )(place, pairs, coeffs, coeffs)


TILE = 256


def collide_kernel(pieces, n_more, last, place, *refs):
    n = len(pieces)
    xs = refs[:n]
    right_own, right_sib, left_own, left_sib = refs[n : n + 4]
    more = refs[n + 4 : n + 4 + n_more]
    out, stacked = refs[n + 4 + n_more :]
    source = pl.program_id(0)
    z, xh = place[0], place[1]

    @pl.when(source == 0)
    def _():
        row = 0
        for x in xs:
            rows = x.shape[0] * x.shape[1] * x.shape[2]
            stacked[pl.ds(row, rows), :] = x[...].reshape(rows, x.shape[3])
            row += rows

    def work(right, left):
        cells = right.shape[1]
        for p in range(2):
            for t in range(cells // TILE):
                at = pl.ds(t * TILE, TILE)
                inner = lax.dot_general(
                    stacked[...],
                    right[p, at, :],
                    (((1,), (1,)), ((), ())),
                    preferred_element_type=jnp.float32,
                )
                sums = [None] * MODES_HERE
                row = 0
                for x, (first, blocks) in zip(xs, pieces):
                    for flip, offset, fixed in blocks:
                        here = fixed if offset is None else lax.rem(z + (offset + Z), Z)
                        column = xh if not flip else 1 - xh
                        factor = left[p, here * XH + column, :, at].astype(jnp.float32)
                        for k in range(x.shape[1]):
                            term = inner[row : row + ROWS] * factor
                            row += ROWS
                            term = (term[0:8] + term[8:16]) + (term[16:24] + term[24:32])
                            m = first + k
                            sums[m] = term if sums[m] is None else sums[m] + term
                done = jnp.concatenate([jnp.sum(s, axis=0, keepdims=True) for s in sums], axis=0)
                for m in more:
                    done = done + m[0, p * MODES_HERE : (p + 1) * MODES_HERE, at]
                if last:
                    for g in range(out.shape[0]):
                        out[g, 0, p * MODES_HERE : (p + 1) * MODES_HERE, at] = done
                else:
                    out[0, p * MODES_HERE : (p + 1) * MODES_HERE, at] = done

    @pl.when(source == 0)
    def _():
        work(right_own, left_own)

    @pl.when(source == 1)
    def _():
        work(right_sib, left_sib)


def collide_part(place, xs, pieces, right_own, right_sib, left_own, left_sib, more=(), last=False):
    _, cells, width = right_own.shape
    rows = sum(x.shape[0] * x.shape[1] * x.shape[2] for x in xs)
    whole = lambda a: pl.BlockSpec(a.shape, lambda s, place: (0,) * a.ndim)
    if last:
        groups = Y * XL
        out_spec = pl.BlockSpec(
            (groups, 1, 2 * MODES_HERE, cells),
            lambda s, place: (0, jnp.where(s == 0, place[2], 1 - place[2]), 0, 0),
        )
        out_shape = jax.ShapeDtypeStruct((groups, CORE, 2 * MODES_HERE, cells), jnp.float32)
    else:
        out_spec = pl.BlockSpec((1, 2 * MODES_HERE, cells), lambda s, place: (s, 0, 0))
        out_shape = jax.ShapeDtypeStruct((2, 2 * MODES_HERE, cells), jnp.float32)
    return pl.pallas_call(
        functools.partial(collide_kernel, pieces, len(more), last),
        grid_spec=pltpu.PrefetchScalarGridSpec(
            num_scalar_prefetch=1,
            grid=(2,),
            in_specs=[whole(a) for a in (*xs, right_own, right_sib, left_own, left_sib)]
            + [pl.BlockSpec((1, 2 * MODES_HERE, cells), lambda s, place: (s, 0, 0)) for _ in more],
            out_specs=out_spec,
            scratch_shapes=[pltpu.VMEM((rows, width), jnp.bfloat16)],
        ),
        out_shape=out_shape,
        compiler_params=pltpu.CompilerParams(vmem_limit_bytes=48 * 2**20),
        cost_estimate=pl.CostEstimate(
            flops=2 * rows * 4 * cells * width, transcendentals=0, bytes_accessed=8 * cells * width
        ),
        name="collide",
    )(place, *xs, right_own, right_sib, left_own, left_sib, *more)


def finish_kernel(pairs, thermal, parts, before, after, window, window_before, window_after, onehot, out, state):
    modes, species, cells = window.shape
    span = cells + 2 * PLANE
    row = lax.broadcasted_iota(jnp.int32, (species, span), 0)
    gain = [
        jnp.where(row == pairs[p, 0], jnp.float32(collision_update), jnp.float32(0.0)) for p in range(2)
    ]
    for g in range(Y * XL):
        own = parts[g, 0] + parts[g, 1]
        both = jnp.concatenate([before[g], own, after[g]], axis=1)
        for k in range(MODES_HERE):
            m = g * MODES_HERE + k
            kept = jnp.concatenate([window_before[m], window[m], window_after[m]], axis=1).astype(jnp.float32)
            for p in range(2):
                r = p * MODES_HERE + k
                kept = kept + gain[p] * both[r : r + 1]
            state[m] = kept
    srow = lax.broadcasted_iota(jnp.int32, (species, cells), 0)
    th = jnp.zeros((species, cells), jnp.float32)
    for s in range(species):
        th = jnp.where(srow == s, thermal[s], th)
    centre = state[:, :, PLANE : PLANE + cells]
    flat = centre.reshape(modes * species, cells)
    high = flat.astype(jnp.bfloat16)
    rest = flat - high.astype(jnp.float32)
    middle = rest.astype(jnp.bfloat16)
    low = (rest - middle.astype(jnp.float32)).astype(jnp.bfloat16)
    pick = onehot[...]
    beside = (
        jnp.dot(low, pick, preferred_element_type=jnp.float32)
        + jnp.dot(middle, pick, preferred_element_type=jnp.float32)
    ) + jnp.dot(high, pick, preferred_element_type=jnp.float32)
    beside = beside.reshape(modes, species, cells)
    for k in range(modes):
        here = state[k, :, PLANE : PLANE + cells]
        ahead = state[k, :, 2 * PLANE :]
        behind = state[k, :, :cells]
        drift = jnp.zeros((species, cells), jnp.float32)
        if k > 0:
            drift += (float(k) ** 0.5) * (state[k - 1, :, 2 * PLANE :] - state[k - 1, :, :cells])
        if k < modes - 1:
            drift += (float(k + 1) ** 0.5) * (state[k + 1, :, 2 * PLANE :] - state[k + 1, :, :cells])
        divergence = th * (0.5 * drift - (0.5 * max_speed) * ((ahead - here) - (here - behind)))
        out[k] = here - courant * divergence + mixing * (beside[k] - here)


def finish(pairs, thermal, parts, before, after, window, window_before, window_after, onehot):
    modes, species, cells = window.shape
    vmem = pl.BlockSpec(memory_space=pltpu.VMEM)
    smem = pl.BlockSpec(memory_space=pltpu.SMEM)
    return pl.pallas_call(
        finish_kernel,
        in_specs=[smem, smem] + [vmem] * 7,
        out_specs=vmem,
        out_shape=jax.ShapeDtypeStruct((modes, species, cells), jnp.float32),
        scratch_shapes=[pltpu.VMEM((modes, species, cells + 2 * PLANE), jnp.float32)],
        compiler_params=pltpu.CompilerParams(vmem_limit_bytes=40 * 2**20),
        name="finish",
    )(pairs, thermal, parts, before, after, window, window_before, window_after, onehot)


def local(coeffs, tensor, pairs, lateral, thermal):
    species, cells, width = coeffs.shape
    modes = tensor.shape[0] * Y * XL
    bricks = Z * XH * CORE
    place = jnp.stack([lax.axis_index("z"), lax.axis_index("xh"), lax.axis_index("core")]).astype(jnp.int32)
    onward = [(i, (i + 1) % bricks) for i in range(bricks)]
    backward = [((i + 1) % bricks, i) for i in range(bricks)]

    column = lax.all_gather(tensor, "z", axis=0, tiled=False)

    other = [lax.ppermute(tensor[2 * h : 2 * h + 2], "xh", SWAP)[None] for h in range(2)]
    right_own, left_own, left_send = prepare(place, pairs, coeffs)
    right_sib = lax.ppermute(right_own, "core", SWAP)
    left_sib = lax.ppermute(left_send, "core", SWAP)

    near, far = [], []
    for h in range(2):
        first = 2 * h
        near.append((other[h], (first, ((True, 0, None),))))
        up = down = other[h]
        for s in range(1, 4 + (h == 0)):
            up = lax.ppermute(up, "z", UP)
            (near if s <= 2 else far).append((up, (first, ((True, -s, None),))))
        for s in range(1, 4 + (h == 1)):
            down = lax.ppermute(down, "z", DOWN)
            (near if s <= 2 else far).append((down, (first, ((True, s, None),))))

    window = jnp.transpose(coeffs[:, :, :modes], (2, 0, 1))
    window_before = lax.ppermute(window[:, :, cells - PLANE :], BRICK, onward)
    window_after = lax.ppermute(window[:, :, :PLANE], BRICK, backward)
    onehot = (lax.broadcasted_iota(jnp.int32, (cells, cells), 0) == lateral[None, :]).astype(jnp.bfloat16)

    sides = (right_own, right_sib, left_own, left_sib)
    part1 = collide_part(place, [a for a, _ in near], tuple(d for _, d in near), *sides)
    part2 = collide_part(place, [a for a, _ in far], tuple(d for _, d in far), *sides)
    whole = (0, tuple((False, None, b) for b in range(Z)))
    parts = collide_part(place, [column], (whole,), *sides, more=(part1, part2), last=True)

    parts = parts.reshape(Y * XL * CORE, 2 * MODES_HERE, cells)
    parts = lax.all_to_all(parts, ("y", "xl", "core"), split_axis=0, concat_axis=0, tiled=True)
    parts = parts.reshape(Y * XL, CORE, 2 * MODES_HERE, cells)
    first = parts[:, 0, :, :PLANE] + parts[:, 1, :, :PLANE]
    final = parts[:, 0, :, cells - PLANE :] + parts[:, 1, :, cells - PLANE :]
    before = lax.ppermute(final, BRICK, onward)
    after = lax.ppermute(first, BRICK, backward)
    return finish(pairs, thermal, parts, before, after, window, window_before, window_after, onehot)


def solution(mesh):
    fine = Mesh(mesh.devices.reshape(Y, XL, Z, XH, CORE), FINE)
    in_specs = (P(None, BRICK, None), P(("y", "xl"), BRICK, None), P(), P(BRICK), P())
    out_specs = P(None, None, BRICK)
    return jax.shard_map(local, mesh=fine, in_specs=in_specs, out_specs=out_specs, check_vma=False)
```

```python
import functools

import jax
import jax.numpy as jnp
from jax import lax
from jax.experimental import pallas as pl
from jax.experimental.pallas import tpu as pltpu
from jax.sharding import Mesh, PartitionSpec as P

PLANE = 128
Y, XL, Z, XH, CORE = 4, 2, 8, 2, 2
FINE = ("y", "xl", "z", "xh", "core")
BRICK = ("z", "xh", "core")
MODES_HERE = 4
ROWS = 32

collision_update = 0.5
courant = 0.08
max_speed = 11.0
mixing = 0.2

UP = [(i, (i + 1) % Z) for i in range(Z)]
DOWN = [((i + 1) % Z, i) for i in range(Z)]
SWAP = [(0, 1), (1, 0)]


def prepare_kernel(pairs, coeffs, right_out, left_out, left, sems):
    copies = []
    for p in range(2):
        copies.append(pltpu.make_async_copy(coeffs.at[pairs[p, 0]], left.at[p], sems.at[p]))
        copies.append(pltpu.make_async_copy(coeffs.at[pairs[p, 1]], right_out.at[p], sems.at[2 + p]))
    for c in copies:
        c.start()
    for p in range(2):
        copies[2 * p].wait()
        left_out[p] = jnp.transpose(left[p]).reshape(left_out.shape[1:])
    for p in range(2):
        copies[2 * p + 1].wait()


VMEM = pl.BlockSpec(memory_space=pltpu.VMEM)
SMEM = pl.BlockSpec(memory_space=pltpu.SMEM)


def prepare(pairs, coeffs):
    _, cells, width = coeffs.shape
    return pl.pallas_call(
        prepare_kernel,
        in_specs=[SMEM, pl.BlockSpec(memory_space=pltpu.HBM)],
        out_specs=[VMEM] * 2,
        out_shape=[
            jax.ShapeDtypeStruct((2, cells, width), coeffs.dtype),
            jax.ShapeDtypeStruct((2, width // ROWS, ROWS, cells), coeffs.dtype),
        ],
        scratch_shapes=[pltpu.VMEM((2, cells, width), coeffs.dtype), pltpu.SemaphoreType.DMA((4,))],
        compiler_params=pltpu.CompilerParams(vmem_limit_bytes=8 * 2**20),
        cost_estimate=pl.CostEstimate(flops=0, transcendentals=0, bytes_accessed=14 * 2**20),
        name="prepare",
    )(pairs, pltpu.with_memory_space_constraint(coeffs, pltpu.HBM))


def window_kernel(pairs, thermal, coeffs, window, gain, heat, rows, sems):
    modes, species, cells = window.shape
    copies = [
        pltpu.make_async_copy(coeffs.at[s, :, pl.ds(0, PLANE)], rows.at[s], sems.at[s]) for s in range(species)
    ]
    for c in copies:
        c.start()
    at = lax.broadcasted_iota(jnp.int32, (species, PLANE), 0)
    for p in range(2):
        gain[p] = jnp.where(at == pairs[p, 0], jnp.float32(collision_update), jnp.float32(0.0))
    speed = jnp.zeros((species, PLANE), jnp.float32)
    for s in range(species):
        speed = jnp.where(at == s, thermal[s], speed)
    heat[...] = speed
    for s in range(species):
        copies[s].wait()
        window[:, s, :] = jnp.transpose(rows[s].astype(jnp.float32))[:modes]


def make_window(pairs, thermal, coeffs, modes):
    species, cells, _ = coeffs.shape
    return pl.pallas_call(
        window_kernel,
        in_specs=[SMEM, SMEM, pl.BlockSpec(memory_space=pltpu.HBM)],
        out_specs=[VMEM] * 3,
        out_shape=[
            jax.ShapeDtypeStruct((modes, species, cells), jnp.float32),
            jax.ShapeDtypeStruct((2, species, PLANE), jnp.float32),
            jax.ShapeDtypeStruct((species, PLANE), jnp.float32),
        ],
        scratch_shapes=[pltpu.VMEM((species, cells, PLANE), coeffs.dtype), pltpu.SemaphoreType.DMA((species,))],
        compiler_params=pltpu.CompilerParams(vmem_limit_bytes=8 * 2**20),
        cost_estimate=pl.CostEstimate(flops=0, transcendentals=0, bytes_accessed=8 * 2**20),
        name="window",
    )(pairs, thermal, pltpu.with_memory_space_constraint(coeffs, pltpu.HBM))


TILE = 256


def collide_kernel(pieces, n_more, last, *refs):
    n = len(pieces)
    xs = refs[:n]
    rights, lefts = refs[n : n + 2], refs[n + 2 : n + 4]
    more = refs[n + 4 : n + 4 + n_more]
    out, stacked = refs[n + 4 + n_more :]
    z, xh, core = (lax.axis_index(a) for a in BRICK)
    block = MODES_HERE * ROWS
    spots = []
    row = 0
    for x, (column, steps) in zip(xs, pieces):
        rows = x.shape[0] * block
        stacked[row : row + rows, :] = x[...].reshape(rows, x.shape[-1])
        row += rows
        there = lax.rem(z + steps * (2 * core - 1) + Z, Z)
        at_column = 1 - xh if column else xh
        for e in range(x.shape[0]):
            spots.append((there * XH + at_column) * CORE + (core if e == 0 else 1 - core))
    cells = rights[0].shape[1]
    for source in range(2):
        right, left = rights[source], lefts[source]
        slot = core if source == 0 else 1 - core
        for p in range(2):
            for t in range(cells // TILE):
                at = pl.ds(t * TILE, TILE)
                inner = lax.dot_general(
                    stacked[...],
                    right[p, at, :],
                    (((1,), (1,)), ((), ())),
                    preferred_element_type=jnp.float32,
                )
                sums = [None] * MODES_HERE
                row = 0
                for spot in spots:
                    factor = left[p, spot, :, at].astype(jnp.float32)
                    for k in range(MODES_HERE):
                        term = inner[row : row + ROWS] * factor
                        row += ROWS
                        term = (term[0:8] + term[8:16]) + (term[16:24] + term[24:32])
                        sums[k] = term if sums[k] is None else sums[k] + term
                done = jnp.concatenate([jnp.sum(s, axis=0, keepdims=True) for s in sums], axis=0)
                kp = slice(p * MODES_HERE, (p + 1) * MODES_HERE)
                for m in more:
                    done = done + m[source, kp, at]
                if last:
                    for g in range(out.shape[0]):
                        out[g, slot, kp, at] = done
                else:
                    out[source, kp, at] = done


def collide_part(xs, pieces, sides, more=(), last=False):
    _, cells, width = sides[0].shape
    rows = sum(x.shape[0] for x in xs) * MODES_HERE * ROWS
    lead = (Y * XL, CORE) if last else (CORE,)
    return pl.pallas_call(
        functools.partial(collide_kernel, pieces, len(more), last),
        in_specs=[VMEM] * (len(xs) + 4 + len(more)),
        out_specs=VMEM,
        out_shape=jax.ShapeDtypeStruct((*lead, 2 * MODES_HERE, cells), jnp.float32),
        scratch_shapes=[pltpu.VMEM((rows, width), jnp.bfloat16)],
        compiler_params=pltpu.CompilerParams(vmem_limit_bytes=8 * 2**20),
        cost_estimate=pl.CostEstimate(
            flops=2 * rows * 4 * cells * width, transcendentals=0, bytes_accessed=8 * cells * width
        ),
        name="collide",
    )(*xs, *sides, *more)


def state_kernel(parts, window, gain, state, first, last):
    modes, species, cells = window.shape
    for g in range(Y * XL):
        own = parts[g, 0] + parts[g, 1]
        for k in range(MODES_HERE):
            m = g * MODES_HERE + k
            for t in range(cells // PLANE):
                at = slice(t * PLANE, (t + 1) * PLANE)
                value = window[m, :, at]
                for p in range(2):
                    r = p * MODES_HERE + k
                    value = value + gain[p] * own[r : r + 1, at]
                state[m, :, at] = value
                if t == 0:
                    first[m] = value
                if t == cells // PLANE - 1:
                    last[m] = value


def root(k):
    return float(k) ** 0.5


def inner_kernel(state, heat, onehot, out):
    modes, species, cells = state.shape
    flat = state[...].reshape(modes * species, cells)
    high = flat.astype(jnp.bfloat16)
    rest = flat - high.astype(jnp.float32)
    middle = rest.astype(jnp.bfloat16)
    low = (rest - middle.astype(jnp.float32)).astype(jnp.bfloat16)
    pick = onehot[...]
    beside = (
        jnp.dot(low, pick, preferred_element_type=jnp.float32)
        + jnp.dot(middle, pick, preferred_element_type=jnp.float32)
    ) + jnp.dot(high, pick, preferred_element_type=jnp.float32)
    out[...] = beside.reshape(modes, species, cells)
    layers = cells // PLANE
    scale = courant * heat[...]

    def drift(k, at):
        total = None
        for j, c in ((k - 1, k), (k + 1, k + 1)):
            if 0 <= j < modes:
                term = root(c) * state[j, :, at]
                total = term if total is None else total + term
        return total

    for k in range(modes):
        for t in range(layers):
            at = slice(t * PLANE, (t + 1) * PLANE)
            here = state[k, :, at]
            divergence = (max_speed * 1.0) * here
            if t + 1 < layers:
                ahead = slice((t + 1) * PLANE, (t + 2) * PLANE)
                divergence += 0.5 * drift(k, ahead) - (0.5 * max_speed) * state[k, :, ahead]
            if t > 0:
                behind = slice((t - 1) * PLANE, t * PLANE)
                divergence -= 0.5 * drift(k, behind) + (0.5 * max_speed) * state[k, :, behind]
            out[k, :, at] = here - scale * divergence + mixing * (out[k, :, at] - here)


def outer_kernel(inner, heat, before, behind, out):
    modes, species, cells = inner.shape
    scale = courant * heat[...]
    for k in range(modes):
        for side, at, sign in ((before, slice(0, PLANE), -1.0), (behind, slice(cells - PLANE, cells), 1.0)):
            divergence = -(0.5 * max_speed) * side[k]
            if k > 0:
                divergence += (sign * 0.5 * root(k)) * side[k - 1]
            if k < modes - 1:
                divergence += (sign * 0.5 * root(k + 1)) * side[k + 1]
            out[k, :, at] = inner[k, :, at] - scale * divergence
        middle = slice(PLANE, cells - PLANE)
        out[k, :, middle] = inner[k, :, middle]


def simple_call(kernel, name, shapes, *operands):
    return pl.pallas_call(
        kernel,
        in_specs=[VMEM] * len(operands),
        out_specs=[VMEM] * len(shapes),
        out_shape=[jax.ShapeDtypeStruct(s, jnp.float32) for s in shapes],
        compiler_params=pltpu.CompilerParams(vmem_limit_bytes=8 * 2**20),
        name=name,
    )(*operands)


def together(*values):
    return lax.optimization_barrier(values)


def local(coeffs, tensor, pairs, lateral, thermal):
    species, cells, width = coeffs.shape
    modes = tensor.shape[0] * Y * XL
    bricks = Z * XH * CORE
    onward = [(i, (i + 1) % bricks) for i in range(bricks)]
    backward = [((i + 1) % bricks, i) for i in range(bricks)]

    ring = [(CORE * i, CORE * ((i + 1) % Z)) for i in range(Z)] + [(CORE * ((i + 1) % Z) + 1, CORE * i + 1) for i in range(Z)]
    step = lambda a: lax.ppermute(a, ("z", "core"), ring)
    both = lambda a: jnp.concatenate([a, lax.ppermute(a, "core", SWAP)])

    tensor = tensor[None]
    other = lax.ppermute(tensor, "xh", SWAP)
    own0 = both(tensor)
    right_own, left_own = prepare(pairs, coeffs)
    own1 = step(own0)
    right_send, left_send = together(right_own, left_own, own0)[:2]
    right_sib = lax.ppermute(right_send, "core", SWAP)
    left_sib = lax.ppermute(left_send, "core", SWAP)
    sides = (right_own, right_sib, left_own, left_sib)
    own1, other = together(own1, other)
    alt1 = step(both(other))
    own2 = step(own1)
    parts = collide_part([tensor, other, own1], [(0, 0), (1, 0), (0, 1)], sides)
    alt1, parts, pairs_now, lateral = together(alt1, parts, pairs, lateral)
    alt2 = step(alt1)
    window, gain, heat = make_window(pairs_now, thermal, coeffs, modes)
    onehot = (lax.broadcasted_iota(jnp.int32, (cells, cells), 0) == lateral[None, :]).astype(jnp.bfloat16)
    own3 = step(own2)
    parts = collide_part([alt1, own2], [(1, 1), (0, 2)], sides, (parts,))
    alt2, parts, window, gain, heat, onehot = together(alt2, parts, window, gain, heat, onehot)
    alt3 = step(alt2)
    own4 = step(own3[:1])
    parts = collide_part([alt2, own3], [(1, 2), (0, 3)], sides, (parts,))
    alt3, parts = together(alt3, parts)
    alt4 = step(alt3[:1])
    parts = collide_part([alt3, own4], [(1, 3), (0, 4)], sides, (parts,))
    parts = collide_part([alt4], [(1, 4)], sides, (parts,), True)

    parts = parts.reshape(Y * XL * CORE, 2 * MODES_HERE, cells)
    parts = lax.all_to_all(parts, ("y", "xl", "core"), split_axis=0, concat_axis=0, tiled=True)
    parts = parts.reshape(Y * XL, CORE, 2 * MODES_HERE, cells)
    full, edge = (modes, species, cells), (modes, species, PLANE)
    state, first, last = simple_call(state_kernel, "state", (full, edge, edge), parts, window, gain)
    before = lax.ppermute(last, BRICK, onward)
    behind = lax.ppermute(first, BRICK, backward)
    inner = simple_call(inner_kernel, "inner", (full,), state, heat, onehot)[0]
    return simple_call(outer_kernel, "outer", (full,), inner, heat, before, behind)[0]


def solution(mesh):
    fine = Mesh(mesh.devices.reshape(Y, XL, Z, XH, CORE), FINE)
    in_specs = (P(None, BRICK, None), P(("y", "xl"), BRICK, None), P(), P(BRICK), P())
    out_specs = P(None, None, BRICK)
    return jax.shard_map(local, mesh=fine, in_specs=in_specs, out_specs=out_specs, check_vma=False)
```

```python
import functools

import jax
import jax.numpy as jnp
from jax import lax
from jax.experimental import pallas as pl
from jax.experimental.pallas import tpu as pltpu
from jax.sharding import Mesh, PartitionSpec as P

PLANE = 128
Y, XL, Z, XH, CORE = 4, 2, 8, 2, 2
FINE = ("y", "xl", "z", "xh", "core")
BRICK = ("z", "xh", "core")
MODES_HERE = 4
ROWS = 32

collision_update = 0.5
courant = 0.08
max_speed = 11.0
mixing = 0.2

UP = [(i, (i + 1) % Z) for i in range(Z)]
DOWN = [((i + 1) % Z, i) for i in range(Z)]
SWAP = [(0, 1), (1, 0)]


BLOCKS = [(0, 0, 0), (1, 0, 0)]
BLOCKS += [(column, swapped, steps) for steps in (1, 2, 3) for column in (0, 1) for swapped in (0, 1)]
BLOCKS += [(0, 0, 4), (1, 0, 4)]


def right_kernel(pairs, coeffs, right_out, sems):
    copies = [pltpu.make_async_copy(coeffs.at[pairs[p, 1]], right_out.at[p], sems.at[p]) for p in range(2)]
    for c in copies:
        c.start()
    for c in copies:
        c.wait()


def left_kernel(pairs, coeffs, keep, give, left, turned, sems):
    copies = [pltpu.make_async_copy(coeffs.at[pairs[p, 0]], left.at[p], sems.at[p]) for p in range(2)]
    for c in copies:
        c.start()
    z, xh, core = (lax.axis_index(a) for a in BRICK)
    for p in range(2):
        copies[p].wait()
        turned[...] = jnp.transpose(left[p]).reshape(turned.shape)
        for out, mine in ((keep, core), (give, 1 - core)):
            for n, (column, swapped, steps) in enumerate(BLOCKS):
                there = lax.rem(z + steps * (2 * mine - 1) + Z, Z)
                column_there = 1 - xh if column else xh
                core_there = 1 - mine if swapped else mine
                out[p, n] = turned[(there * XH + column_there) * CORE + core_there]


VMEM = pl.BlockSpec(memory_space=pltpu.VMEM)
SMEM = pl.BlockSpec(memory_space=pltpu.SMEM)


def make_right(pairs, coeffs):
    _, cells, width = coeffs.shape
    return pl.pallas_call(
        right_kernel,
        in_specs=[SMEM, pl.BlockSpec(memory_space=pltpu.HBM)],
        out_specs=VMEM,
        out_shape=jax.ShapeDtypeStruct((2, cells, width), coeffs.dtype),
        scratch_shapes=[pltpu.SemaphoreType.DMA((2,))],
        compiler_params=pltpu.CompilerParams(vmem_limit_bytes=8 * 2**20),
        cost_estimate=pl.CostEstimate(flops=0, transcendentals=0, bytes_accessed=4 * 2**20),
        name="right",
    )(pairs, pltpu.with_memory_space_constraint(coeffs, pltpu.HBM))


def make_left(pairs, coeffs):
    _, cells, width = coeffs.shape
    blocks = jax.ShapeDtypeStruct((2, len(BLOCKS), ROWS, cells), coeffs.dtype)
    return pl.pallas_call(
        left_kernel,
        in_specs=[SMEM, pl.BlockSpec(memory_space=pltpu.HBM)],
        out_specs=[VMEM] * 2,
        out_shape=[blocks, blocks],
        scratch_shapes=[
            pltpu.VMEM((2, cells, width), coeffs.dtype),
            pltpu.VMEM((width // ROWS, ROWS, cells), coeffs.dtype),
            pltpu.SemaphoreType.DMA((2,)),
        ],
        compiler_params=pltpu.CompilerParams(vmem_limit_bytes=10 * 2**20),
        cost_estimate=pl.CostEstimate(flops=0, transcendentals=0, bytes_accessed=10 * 2**20),
        name="left",
    )(pairs, pltpu.with_memory_space_constraint(coeffs, pltpu.HBM))


def window_kernel(pairs, thermal, coeffs, window, gain, heat, rows, sems):
    modes, species, cells = window.shape
    copies = [
        pltpu.make_async_copy(coeffs.at[s, :, pl.ds(0, PLANE)], rows.at[s], sems.at[s]) for s in range(species)
    ]
    for c in copies:
        c.start()
    at = lax.broadcasted_iota(jnp.int32, (species, PLANE), 0)
    for p in range(2):
        gain[p] = jnp.where(at == pairs[p, 0], jnp.float32(collision_update), jnp.float32(0.0))
    speed = jnp.zeros((species, PLANE), jnp.float32)
    for s in range(species):
        speed = jnp.where(at == s, thermal[s], speed)
    heat[...] = speed
    for s in range(species):
        copies[s].wait()
        window[:, s, :] = jnp.transpose(rows[s].astype(jnp.float32))[:modes]


def make_window(pairs, thermal, coeffs, modes):
    species, cells, _ = coeffs.shape
    return pl.pallas_call(
        window_kernel,
        in_specs=[SMEM, SMEM, pl.BlockSpec(memory_space=pltpu.HBM)],
        out_specs=[VMEM] * 3,
        out_shape=[
            jax.ShapeDtypeStruct((modes, species, cells), jnp.float32),
            jax.ShapeDtypeStruct((2, species, PLANE), jnp.float32),
            jax.ShapeDtypeStruct((species, PLANE), jnp.float32),
        ],
        scratch_shapes=[pltpu.VMEM((species, cells, PLANE), coeffs.dtype), pltpu.SemaphoreType.DMA((species,))],
        compiler_params=pltpu.CompilerParams(vmem_limit_bytes=8 * 2**20),
        cost_estimate=pl.CostEstimate(flops=0, transcendentals=0, bytes_accessed=8 * 2**20),
        name="window",
    )(pairs, thermal, pltpu.with_memory_space_constraint(coeffs, pltpu.HBM))


TILE = 256


def collide_kernel(pieces, n_more, last, *refs):
    n = len(pieces)
    xs = refs[:n]
    rights, lefts = refs[n : n + 2], refs[n + 2 : n + 4]
    more = refs[n + 4 : n + 4 + n_more]
    out, stacked = refs[n + 4 + n_more :]
    core = lax.axis_index("core")
    block = MODES_HERE * ROWS
    spots = []
    row = 0
    for x, (column, steps) in zip(xs, pieces):
        rows = x.shape[0] * block
        stacked[row : row + rows, :] = x[...].reshape(rows, x.shape[-1])
        row += rows
        spots += [BLOCKS.index((column, e, steps)) for e in range(x.shape[0])]
    cells = rights[0].shape[1]
    for source in range(2):
        right, left = rights[source], lefts[source]
        slot = core if source == 0 else 1 - core
        for p in range(2):
            for t in range(cells // TILE):
                at = pl.ds(t * TILE, TILE)
                inner = lax.dot_general(
                    stacked[...],
                    right[p, at, :],
                    (((1,), (1,)), ((), ())),
                    preferred_element_type=jnp.float32,
                )
                sums = [None] * MODES_HERE
                row = 0
                for spot in spots:
                    factor = left[p, spot, :, at].astype(jnp.float32)
                    for k in range(MODES_HERE):
                        term = inner[row : row + ROWS] * factor
                        row += ROWS
                        term = (term[0:8] + term[8:16]) + (term[16:24] + term[24:32])
                        sums[k] = term if sums[k] is None else sums[k] + term
                done = jnp.concatenate([jnp.sum(s, axis=0, keepdims=True) for s in sums], axis=0)
                kp = slice(p * MODES_HERE, (p + 1) * MODES_HERE)
                for m in more:
                    done = done + m[source, kp, at]
                if last:
                    for g in range(out.shape[0]):
                        out[g, slot, kp, at] = done
                else:
                    out[source, kp, at] = done


def collide_part(xs, pieces, sides, more=(), last=False):
    _, cells, width = sides[0].shape
    rows = sum(x.shape[0] for x in xs) * MODES_HERE * ROWS
    lead = (Y * XL, CORE) if last else (CORE,)
    return pl.pallas_call(
        functools.partial(collide_kernel, pieces, len(more), last),
        in_specs=[VMEM] * (len(xs) + 4 + len(more)),
        out_specs=VMEM,
        out_shape=jax.ShapeDtypeStruct((*lead, 2 * MODES_HERE, cells), jnp.float32),
        scratch_shapes=[pltpu.VMEM((rows, width), jnp.bfloat16)],
        compiler_params=pltpu.CompilerParams(vmem_limit_bytes=8 * 2**20),
        cost_estimate=pl.CostEstimate(
            flops=2 * rows * 4 * cells * width, transcendentals=0, bytes_accessed=8 * cells * width
        ),
        name="collide",
    )(*xs, *sides, *more)


def state_kernel(parts, window, gain, state, inward, outward):
    modes, species, cells = window.shape
    core = lax.axis_index("core")
    for g in range(Y * XL):
        own = parts[g, 0] + parts[g, 1]
        for k in range(MODES_HERE):
            m = g * MODES_HERE + k
            for t in range(cells // PLANE):
                at = slice(t * PLANE, (t + 1) * PLANE)
                value = window[m, :, at]
                for p in range(2):
                    r = p * MODES_HERE + k
                    value = value + gain[p] * own[r : r + 1, at]
                state[m, :, at] = value
    first, last = slice(0, PLANE), slice(cells - PLANE, cells)

    @pl.when(core == 0)
    def _():
        inward[...] = state[:, :, last]
        outward[...] = state[:, :, first]

    @pl.when(core == 1)
    def _():
        inward[...] = state[:, :, first]
        outward[...] = state[:, :, last]


def root(k):
    return float(k) ** 0.5


def inner_kernel(state, heat, onehot, out):
    modes, species, cells = state.shape
    flat = state[...].reshape(modes * species, cells)
    high = flat.astype(jnp.bfloat16)
    rest = flat - high.astype(jnp.float32)
    middle = rest.astype(jnp.bfloat16)
    low = (rest - middle.astype(jnp.float32)).astype(jnp.bfloat16)
    pick = onehot[...]
    beside = (
        jnp.dot(low, pick, preferred_element_type=jnp.float32)
        + jnp.dot(middle, pick, preferred_element_type=jnp.float32)
    ) + jnp.dot(high, pick, preferred_element_type=jnp.float32)
    out[...] = beside.reshape(modes, species, cells)
    layers = cells // PLANE
    scale = courant * heat[...]

    def drift(k, at):
        total = None
        for j, c in ((k - 1, k), (k + 1, k + 1)):
            if 0 <= j < modes:
                term = root(c) * state[j, :, at]
                total = term if total is None else total + term
        return total

    for k in range(modes):
        for t in range(layers):
            at = slice(t * PLANE, (t + 1) * PLANE)
            here = state[k, :, at]
            divergence = (max_speed * 1.0) * here
            if t + 1 < layers:
                ahead = slice((t + 1) * PLANE, (t + 2) * PLANE)
                divergence += 0.5 * drift(k, ahead) - (0.5 * max_speed) * state[k, :, ahead]
            if t > 0:
                behind = slice((t - 1) * PLANE, t * PLANE)
                divergence -= 0.5 * drift(k, behind) + (0.5 * max_speed) * state[k, :, behind]
            out[k, :, at] = here - scale * divergence + mixing * (out[k, :, at] - here)


def outer_kernel(inner, heat, inward, outward, out):
    modes, species, cells = inner.shape
    core = lax.axis_index("core")
    scale = courant * heat[...]

    def work(before, behind):
        for k in range(modes):
            for side, at, sign in ((before, slice(0, PLANE), -1.0), (behind, slice(cells - PLANE, cells), 1.0)):
                divergence = -(0.5 * max_speed) * side[k]
                if k > 0:
                    divergence += (sign * 0.5 * root(k)) * side[k - 1]
                if k < modes - 1:
                    divergence += (sign * 0.5 * root(k + 1)) * side[k + 1]
                out[k, :, at] = inner[k, :, at] - scale * divergence
            middle = slice(PLANE, cells - PLANE)
            out[k, :, middle] = inner[k, :, middle]

    @pl.when(core == 0)
    def _():
        work(outward, inward)

    @pl.when(core == 1)
    def _():
        work(inward, outward)


def simple_call(kernel, name, shapes, *operands):
    return pl.pallas_call(
        kernel,
        in_specs=[VMEM] * len(operands),
        out_specs=[VMEM] * len(shapes),
        out_shape=[jax.ShapeDtypeStruct(s, jnp.float32) for s in shapes],
        compiler_params=pltpu.CompilerParams(vmem_limit_bytes=8 * 2**20),
        name=name,
    )(*operands)


def together(*values):
    return lax.optimization_barrier(values)


def local(coeffs, tensor, pairs, lateral, thermal):
    species, cells, width = coeffs.shape
    modes = tensor.shape[0] * Y * XL
    bricks = Z * XH * CORE

    ring = [(CORE * i, CORE * ((i + 1) % Z)) for i in range(Z)] + [(CORE * ((i + 1) % Z) + 1, CORE * i + 1) for i in range(Z)]
    step = lambda a: lax.ppermute(a, ("z", "core"), ring)
    both = lambda a: jnp.concatenate([a, lax.ppermute(a, "core", SWAP)])

    tensor = tensor[None]
    other = lax.ppermute(tensor, "xh", SWAP)
    own0 = both(tensor)
    pairs_now = together(pairs, own0)[0]
    right_own = make_right(pairs_now, coeffs)
    left_own, left_send = make_left(pairs_now, coeffs)
    own1 = step(own0)
    own1, other, right_own, left_own, left_send = together(own1, other, right_own, left_own, left_send)
    alt0 = both(other)
    alt1 = step(alt0)
    own2 = step(own1)
    right_send, left_send = together(right_own, left_send, alt0)[:2]
    right_sib = lax.ppermute(right_send, "core", SWAP)
    left_sib = lax.ppermute(left_send, "core", SWAP)
    sides = (right_own, right_sib, left_own, left_sib)
    pairs_now, lateral = together(pairs, lateral, alt0)[:2]
    window, gain, heat = make_window(pairs_now, thermal, coeffs, modes)
    onehot = (lax.broadcasted_iota(jnp.int32, (cells, cells), 0) == lateral[None, :]).astype(jnp.bfloat16)
    alt1, right_sib, left_sib, window, gain, heat, onehot = together(
        alt1, right_sib, left_sib, window, gain, heat, onehot
    )
    sides = (right_own, right_sib, left_own, left_sib)
    alt2 = step(alt1)
    own3 = step(own2)
    parts = collide_part([tensor, other, own1], [(0, 0), (1, 0), (0, 1)], sides)
    alt2, parts = together(alt2, parts)
    alt3 = step(alt2)
    own4 = step(own3[:1])
    parts = collide_part([alt1, own2], [(1, 1), (0, 2)], sides, (parts,))
    alt3, parts = together(alt3, parts)
    alt4 = step(alt3[:1])
    parts = collide_part([alt2, own3], [(1, 2), (0, 3)], sides, (parts,))
    parts = collide_part([alt3, own4], [(1, 3), (0, 4)], sides, (parts,))
    parts = collide_part([alt4], [(1, 4)], sides, (parts,), True)

    parts = parts.reshape(Y * XL * CORE, 2 * MODES_HERE, cells)
    parts = lax.all_to_all(parts, ("y", "xl", "core"), split_axis=0, concat_axis=0, tiled=True)
    parts = parts.reshape(Y * XL, CORE, 2 * MODES_HERE, cells)
    full, edge = (modes, species, cells), (modes, species, PLANE)
    state, inward, outward = simple_call(state_kernel, "state", (full, edge, edge), parts, window, gain)
    facing = [(i, (i + 1 if i % 2 else i - 1) % bricks) for i in range(bricks)]
    outward = lax.ppermute(outward, BRICK, facing)
    inward = lax.ppermute(inward, "core", SWAP)
    inner = simple_call(inner_kernel, "inner", (full,), state, heat, onehot)[0]
    return simple_call(outer_kernel, "outer", (full,), inner, heat, inward, outward)[0]


def solution(mesh):
    fine = Mesh(mesh.devices.reshape(Y, XL, Z, XH, CORE), FINE)
    in_specs = (P(None, BRICK, None), P(("y", "xl"), BRICK, None), P(), P(BRICK), P())
    out_specs = P(None, None, BRICK)
    return jax.shard_map(local, mesh=fine, in_specs=in_specs, out_specs=out_specs, check_vma=False)
```

```python
import functools

import jax
import jax.numpy as jnp
from jax import lax
from jax.experimental import pallas as pl
from jax.experimental.pallas import tpu as pltpu
from jax.sharding import Mesh, PartitionSpec as P

PLANE = 128
Y, XL, Z, XH, CORE = 4, 2, 8, 2, 2
FINE = ("y", "xl", "z", "xh", "core")
BRICK = ("z", "xh", "core")
MODES_HERE = 4
ROWS = 32

collision_update = 0.5
courant = 0.08
max_speed = 11.0
mixing = 0.2

UP = [(i, (i + 1) % Z) for i in range(Z)]
DOWN = [((i + 1) % Z, i) for i in range(Z)]
SWAP = [(0, 1), (1, 0)]


BLOCKS = [(0, 0, 0), (1, 0, 0)]
BLOCKS += [(column, swapped, steps) for steps in (1, 2, 3) for column in (0, 1) for swapped in (0, 1)]
BLOCKS += [(0, 0, 4), (1, 0, 4)]


def right_kernel(pairs, coeffs, right_out, sems):
    copies = [pltpu.make_async_copy(coeffs.at[pairs[p, 1]], right_out.at[p], sems.at[p]) for p in range(2)]
    for c in copies:
        c.start()
    for c in copies:
        c.wait()


def left_kernel(pairs, coeffs, keep, give, left, turned, sems):
    copies = [pltpu.make_async_copy(coeffs.at[pairs[p, 0]], left.at[p], sems.at[p]) for p in range(2)]
    for c in copies:
        c.start()
    z, xh, core = (lax.axis_index(a) for a in BRICK)
    for p in range(2):
        copies[p].wait()
        turned[...] = jnp.transpose(left[p]).reshape(turned.shape)
        for out, mine in ((keep, core), (give, 1 - core)):
            for n, (column, swapped, steps) in enumerate(BLOCKS):
                there = lax.rem(z + steps * (2 * mine - 1) + Z, Z)
                column_there = 1 - xh if column else xh
                core_there = 1 - mine if swapped else mine
                out[p, n] = turned[(there * XH + column_there) * CORE + core_there]


VMEM = pl.BlockSpec(memory_space=pltpu.VMEM)
SMEM = pl.BlockSpec(memory_space=pltpu.SMEM)


def make_right(pairs, coeffs):
    _, cells, width = coeffs.shape
    return pl.pallas_call(
        right_kernel,
        in_specs=[SMEM, pl.BlockSpec(memory_space=pltpu.HBM)],
        out_specs=VMEM,
        out_shape=jax.ShapeDtypeStruct((2, cells, width), coeffs.dtype),
        scratch_shapes=[pltpu.SemaphoreType.DMA((2,))],
        compiler_params=pltpu.CompilerParams(vmem_limit_bytes=8 * 2**20),
        cost_estimate=pl.CostEstimate(flops=0, transcendentals=0, bytes_accessed=4 * 2**20),
        name="right",
    )(pairs, pltpu.with_memory_space_constraint(coeffs, pltpu.HBM))


def make_left(pairs, coeffs):
    _, cells, width = coeffs.shape
    blocks = jax.ShapeDtypeStruct((2, len(BLOCKS), ROWS, cells), coeffs.dtype)
    return pl.pallas_call(
        left_kernel,
        in_specs=[SMEM, pl.BlockSpec(memory_space=pltpu.HBM)],
        out_specs=[VMEM] * 2,
        out_shape=[blocks, blocks],
        scratch_shapes=[
            pltpu.VMEM((2, cells, width), coeffs.dtype),
            pltpu.VMEM((width // ROWS, ROWS, cells), coeffs.dtype),
            pltpu.SemaphoreType.DMA((2,)),
        ],
        compiler_params=pltpu.CompilerParams(vmem_limit_bytes=10 * 2**20),
        cost_estimate=pl.CostEstimate(flops=0, transcendentals=0, bytes_accessed=10 * 2**20),
        name="left",
    )(pairs, pltpu.with_memory_space_constraint(coeffs, pltpu.HBM))


def window_kernel(pairs, thermal, coeffs, window, gain, heat, rows, sems):
    modes, species, cells = window.shape
    copies = [
        pltpu.make_async_copy(coeffs.at[s, :, pl.ds(0, PLANE)], rows.at[s], sems.at[s]) for s in range(species)
    ]
    for c in copies:
        c.start()
    at = lax.broadcasted_iota(jnp.int32, (species, PLANE), 0)
    for p in range(2):
        gain[p] = jnp.where(at == pairs[p, 0], jnp.float32(collision_update), jnp.float32(0.0))
    speed = jnp.zeros((species, PLANE), jnp.float32)
    for s in range(species):
        speed = jnp.where(at == s, thermal[s], speed)
    heat[...] = speed
    for s in range(species):
        copies[s].wait()
        window[:, s, :] = jnp.transpose(rows[s].astype(jnp.float32))[:modes]


def make_window(pairs, thermal, coeffs, modes):
    species, cells, _ = coeffs.shape
    return pl.pallas_call(
        window_kernel,
        in_specs=[SMEM, SMEM, pl.BlockSpec(memory_space=pltpu.HBM)],
        out_specs=[VMEM] * 3,
        out_shape=[
            jax.ShapeDtypeStruct((modes, species, cells), jnp.float32),
            jax.ShapeDtypeStruct((2, species, PLANE), jnp.float32),
            jax.ShapeDtypeStruct((species, PLANE), jnp.float32),
        ],
        scratch_shapes=[pltpu.VMEM((species, cells, PLANE), coeffs.dtype), pltpu.SemaphoreType.DMA((species,))],
        compiler_params=pltpu.CompilerParams(vmem_limit_bytes=8 * 2**20),
        cost_estimate=pl.CostEstimate(flops=0, transcendentals=0, bytes_accessed=8 * 2**20),
        name="window",
    )(pairs, thermal, pltpu.with_memory_space_constraint(coeffs, pltpu.HBM))


TILE = 256


def collide_kernel(pieces, n_more, last, *refs):
    n = len(pieces)
    xs = refs[:n]
    rights, lefts = refs[n : n + 2], refs[n + 2 : n + 4]
    more = refs[n + 4 : n + 4 + n_more]
    out, stacked = refs[n + 4 + n_more :]
    core = lax.axis_index("core")
    block = MODES_HERE * ROWS
    for n, x in enumerate(xs):
        stacked[n * block : (n + 1) * block, :] = x[...].reshape(block, x.shape[-1])
    spots = [BLOCKS.index(piece) for piece in pieces]
    cells = rights[0].shape[1]
    for source in range(2):
        right, left = rights[source], lefts[source]
        slot = core if source == 0 else 1 - core
        for p in range(2):
            for t in range(cells // TILE):
                at = pl.ds(t * TILE, TILE)
                inner = lax.dot_general(
                    stacked[...],
                    right[p, at, :],
                    (((1,), (1,)), ((), ())),
                    preferred_element_type=jnp.float32,
                )
                sums = [None] * MODES_HERE
                row = 0
                for spot in spots:
                    factor = left[p, spot, :, at].astype(jnp.float32)
                    for k in range(MODES_HERE):
                        term = inner[row : row + ROWS] * factor
                        row += ROWS
                        term = (term[0:8] + term[8:16]) + (term[16:24] + term[24:32])
                        sums[k] = term if sums[k] is None else sums[k] + term
                done = jnp.concatenate([jnp.sum(s, axis=0, keepdims=True) for s in sums], axis=0)
                kp = slice(p * MODES_HERE, (p + 1) * MODES_HERE)
                for m in more:
                    done = done + m[source, kp, at]
                if last:
                    for g in range(out.shape[0]):
                        out[g, slot, kp, at] = done
                else:
                    out[source, kp, at] = done


def collide_part(xs, pieces, sides, more=(), last=False):
    _, cells, width = sides[0].shape
    rows = len(xs) * MODES_HERE * ROWS
    lead = (Y * XL, CORE) if last else (CORE,)
    return pl.pallas_call(
        functools.partial(collide_kernel, pieces, len(more), last),
        in_specs=[VMEM] * (len(xs) + 4 + len(more)),
        out_specs=VMEM,
        out_shape=jax.ShapeDtypeStruct((*lead, 2 * MODES_HERE, cells), jnp.float32),
        scratch_shapes=[pltpu.VMEM((rows, width), jnp.bfloat16)],
        compiler_params=pltpu.CompilerParams(vmem_limit_bytes=8 * 2**20),
        cost_estimate=pl.CostEstimate(
            flops=2 * rows * 4 * cells * width, transcendentals=0, bytes_accessed=8 * cells * width
        ),
        name="collide",
    )(*xs, *sides, *more)


def state_kernel(parts, window, gain, state, inward, outward):
    modes, species, cells = window.shape
    core = lax.axis_index("core")
    for g in range(Y * XL):
        own = parts[g, 0] + parts[g, 1]
        for k in range(MODES_HERE):
            m = g * MODES_HERE + k
            for t in range(cells // PLANE):
                at = slice(t * PLANE, (t + 1) * PLANE)
                value = window[m, :, at]
                for p in range(2):
                    r = p * MODES_HERE + k
                    value = value + gain[p] * own[r : r + 1, at]
                state[m, :, at] = value
    first, last = slice(0, PLANE), slice(cells - PLANE, cells)

    @pl.when(core == 0)
    def _():
        inward[...] = state[:, :, last]
        outward[...] = state[:, :, first]

    @pl.when(core == 1)
    def _():
        inward[...] = state[:, :, first]
        outward[...] = state[:, :, last]


def root(k):
    return float(k) ** 0.5


def inner_kernel(state, heat, onehot, out):
    modes, species, cells = state.shape
    flat = state[...].reshape(modes * species, cells)
    high = flat.astype(jnp.bfloat16)
    rest = flat - high.astype(jnp.float32)
    middle = rest.astype(jnp.bfloat16)
    low = (rest - middle.astype(jnp.float32)).astype(jnp.bfloat16)
    pick = onehot[...]
    beside = (
        jnp.dot(low, pick, preferred_element_type=jnp.float32)
        + jnp.dot(middle, pick, preferred_element_type=jnp.float32)
    ) + jnp.dot(high, pick, preferred_element_type=jnp.float32)
    out[...] = beside.reshape(modes, species, cells)
    layers = cells // PLANE
    scale = courant * heat[...]

    def drift(k, at):
        total = None
        for j, c in ((k - 1, k), (k + 1, k + 1)):
            if 0 <= j < modes:
                term = root(c) * state[j, :, at]
                total = term if total is None else total + term
        return total

    for k in range(modes):
        for t in range(layers):
            at = slice(t * PLANE, (t + 1) * PLANE)
            here = state[k, :, at]
            divergence = (max_speed * 1.0) * here
            if t + 1 < layers:
                ahead = slice((t + 1) * PLANE, (t + 2) * PLANE)
                divergence += 0.5 * drift(k, ahead) - (0.5 * max_speed) * state[k, :, ahead]
            if t > 0:
                behind = slice((t - 1) * PLANE, t * PLANE)
                divergence -= 0.5 * drift(k, behind) + (0.5 * max_speed) * state[k, :, behind]
            out[k, :, at] = here - scale * divergence + mixing * (out[k, :, at] - here)


def outer_kernel(inner, heat, inward, outward, out):
    modes, species, cells = inner.shape
    core = lax.axis_index("core")
    scale = courant * heat[...]

    def work(before, behind):
        for k in range(modes):
            for side, at, sign in ((before, slice(0, PLANE), -1.0), (behind, slice(cells - PLANE, cells), 1.0)):
                divergence = -(0.5 * max_speed) * side[k]
                if k > 0:
                    divergence += (sign * 0.5 * root(k)) * side[k - 1]
                if k < modes - 1:
                    divergence += (sign * 0.5 * root(k + 1)) * side[k + 1]
                out[k, :, at] = inner[k, :, at] - scale * divergence
            middle = slice(PLANE, cells - PLANE)
            out[k, :, middle] = inner[k, :, middle]

    @pl.when(core == 0)
    def _():
        work(outward, inward)

    @pl.when(core == 1)
    def _():
        work(inward, outward)


def simple_call(kernel, name, shapes, *operands):
    return pl.pallas_call(
        kernel,
        in_specs=[VMEM] * len(operands),
        out_specs=[VMEM] * len(shapes),
        out_shape=[jax.ShapeDtypeStruct(s, jnp.float32) for s in shapes],
        compiler_params=pltpu.CompilerParams(vmem_limit_bytes=8 * 2**20),
        name=name,
    )(*operands)


def together(*values):
    return lax.optimization_barrier(values)


def local(coeffs, tensor, pairs, lateral, thermal):
    species, cells, width = coeffs.shape
    modes = tensor.shape[0] * Y * XL
    bricks = Z * XH * CORE

    ring = [(CORE * i, CORE * ((i + 1) % Z)) for i in range(Z)] + [(CORE * ((i + 1) % Z) + 1, CORE * i + 1) for i in range(Z)]
    step = lambda a: lax.ppermute(a, ("z", "core"), ring)
    swap = lambda a: lax.ppermute(a, "core", SWAP)

    got = {}

    def part(keys, more=(), last=False):
        return collide_part([got[key] for key in keys], keys, sides, more, last)

    def send(column, swapped, steps):
        got[column, swapped, steps] = step(got[column, swapped, steps - 1])

    got[0, 0, 0] = tensor
    got[1, 0, 0] = lax.ppermute(tensor, "xh", SWAP)
    got[0, 1, 0] = swap(tensor)
    send(0, 0, 1)
    send(0, 1, 1)
    pairs_now = together(pairs, got[0, 1, 0])[0]
    right_own = make_right(pairs_now, coeffs)
    left_own, left_send = make_left(pairs_now, coeffs)
    got[0, 0, 1], got[0, 1, 1], got[1, 0, 0], right_own, left_own, left_send = together(
        got[0, 0, 1], got[0, 1, 1], got[1, 0, 0], right_own, left_own, left_send
    )
    got[1, 1, 0] = swap(got[1, 0, 0])
    send(0, 0, 2)
    send(1, 0, 1)
    send(0, 1, 2)
    send(1, 1, 1)
    right_send, left_send, pairs_now, lateral = together(right_own, left_send, pairs, lateral, got[1, 1, 0])[:4]
    right_sib, left_sib = swap(right_send), swap(left_send)
    window, gain, heat = make_window(pairs_now, thermal, coeffs, modes)
    onehot = (lax.broadcasted_iota(jnp.int32, (cells, cells), 0) == lateral[None, :]).astype(jnp.bfloat16)
    got[1, 1, 1], right_sib, left_sib, window, gain, heat, onehot = together(
        got[1, 1, 1], right_sib, left_sib, window, gain, heat, onehot
    )
    sides = (right_own, right_sib, left_own, left_sib)
    send(0, 0, 3)
    send(1, 0, 2)
    send(0, 1, 3)
    send(1, 1, 2)
    parts = part([(0, 0, 0), (1, 0, 0), (0, 0, 1), (0, 1, 1)])
    got[1, 1, 2], parts = together(got[1, 1, 2], parts)
    send(1, 0, 3)
    send(1, 1, 3)
    send(0, 0, 4)
    parts = part([(1, 0, 1), (1, 1, 1), (0, 0, 2), (0, 1, 2)], (parts,))
    got[1, 0, 3], parts = together(got[1, 0, 3], parts)
    send(1, 0, 4)
    parts = part([(1, 0, 2), (1, 1, 2), (0, 0, 3), (0, 1, 3)], (parts,))
    parts = part([(1, 0, 3), (1, 1, 3), (0, 0, 4)], (parts,))
    parts = part([(1, 0, 4)], (parts,), True)

    parts = parts.reshape(Y * XL * CORE, 2 * MODES_HERE, cells)
    parts = lax.all_to_all(parts, ("y", "xl", "core"), split_axis=0, concat_axis=0, tiled=True)
    parts = parts.reshape(Y * XL, CORE, 2 * MODES_HERE, cells)
    full, edge = (modes, species, cells), (modes, species, PLANE)
    state, inward, outward = simple_call(state_kernel, "state", (full, edge, edge), parts, window, gain)
    facing = [(i, (i + 1 if i % 2 else i - 1) % bricks) for i in range(bricks)]
    outward = lax.ppermute(outward, BRICK, facing)
    inward = lax.ppermute(inward, "core", SWAP)
    inner = simple_call(inner_kernel, "inner", (full,), state, heat, onehot)[0]
    return simple_call(outer_kernel, "outer", (full,), inner, heat, inward, outward)[0]


def solution(mesh):
    fine = Mesh(mesh.devices.reshape(Y, XL, Z, XH, CORE), FINE)
    in_specs = (P(None, BRICK, None), P(("y", "xl"), BRICK, None), P(), P(BRICK), P())
    out_specs = P(None, None, BRICK)
    return jax.shard_map(local, mesh=fine, in_specs=in_specs, out_specs=out_specs, check_vma=False)
```
